32 devices in a mesh: filt: 16 (over z, y, x), depth: 2 (over core).
Axes of the slice: x: 2, y: 2, z: 4, core: 2. Of those that a mesh axis runs over, the one named last changes fastest.
Arguments:
- volume: bfloat16 [256, 8, 64, 128], P(None, 'depth', 'filt'), may hold values from -6 to 6
- weights: bfloat16 [128, 27, 256], P('filt'), may hold values from -0.078125 to 0.078125
- bias: float32 [128], replicated, may hold values from -3 to 3
- grad_out: bfloat16 [128, 8, 64, 128], P(None, 'depth', 'filt'), may hold values from -0.0234375 to 0.0234375
Outputs:
- output: bfloat16 [128, 8, 64, 128], P(None, 'depth', 'filt')
- grad_w: float32 [128, 27, 256], P('filt')
The draws below stay inside these ranges and needn't reach their ends.
All inputs are finite; a program needn't handle non-finite values.
Results may differ from the reference program's by a relative error of at most 0.001.
Values may be sent and summed in bfloat16 or wider, within the bound.
A program may use at most 64 MiB of HBM per device.

```python
import jax
import jax.numpy as jnp
from jax import lax

CIN = 256
COUT = 128
Y = 128
NZ = 8
X = 64


def spiked(array, own_key, source, target, shards_of, factor):
    owner, partner = [(jnp.arange(array.shape[axis_at]) // (array.shape[axis_at] // shards_of)).reshape([-1 if axis == axis_at else 1 for axis in range(array.ndim)]) for axis_at in (source, target)]
    chosen = jax.random.permutation(own_key, shards_of)[partner]
    strong = (owner == chosen) | (owner == (partner + shards_of // 2) % shards_of)
    return jnp.where(strong, factor * array, array)


def levels(stream_key, dims, shards, smallest, largest):
    gain, own = 1.0, jax.random.fold_in(stream_key, 6)
    for dim, parts in shards:
        draws = jnp.exp(jax.random.uniform(jax.random.fold_in(own, dim), (parts,), jnp.float32, smallest / len(shards), largest / len(shards)))
        gain = gain * jnp.repeat(draws, dims[dim] // parts).reshape([-1 if axis == dim else 1 for axis in range(len(dims))])
    return gain


def centred(own_key, dims, deviation, reach, shards=(), dtype=jnp.bfloat16):
    loudness = levels(own_key, dims, shards, -0.22, 0.18) if shards else 1.0
    drawn = jax.random.normal(own_key, dims, jnp.float32) * deviation * loudness
    return jnp.minimum(jnp.maximum(drawn, -reach), reach).astype(dtype)


def bell_draw_with(stream_key, shape, width, most, shards, heavy, held_as=jnp.bfloat16):
    drawn = width * jax.random.normal(stream_key, shape, jnp.float32)
    if shards:
        drawn = drawn * levels(stream_key, shape, shards, -0.22, 0.18)
    return jnp.clip(spiked(drawn, jax.random.fold_in(stream_key, 3), *heavy), -most, most).astype(held_as)


def setup_inputs(seed: int = 0) -> dict:
    key_of = jax.random.split(jax.random.key(seed), 5)
    return {
        "volume": centred(key_of[0], (CIN, NZ, X, Y), 1.0, 6.0, ((1, 2), (2, 16))),
        "weights": centred(key_of[1], (COUT, 27, CIN), (27 * CIN) ** -0.5, 0.078125, ((0, 16),)),
        "bias": centred(key_of[2], (COUT,), 0.5, 3.0, (), jnp.float32),
        "grad_out": bell_draw_with(key_of[3], (COUT, NZ, X, Y), (1.0 / (X * Y * NZ) ** 0.5), 0.0234375, ((1, 2), (2, 16)), (2, 0, 16, 2.0)),
    }


def reference(volume, weights, bias, grad_out):
    field = volume.astype(jnp.float32)
    kernel = weights.astype(jnp.float32).reshape(COUT, 3, 3, 3, CIN)
    forward = lax.conv_general_dilated(field[None], kernel, (1, 1, 1), ((1, 1), (1, 1), (1, 1)), dimension_numbers=("NCDHW", "ODHWI", "NCDHW"), precision=lax.Precision.HIGHEST)
    output = (forward[0] + bias[:, None, None, None]).astype(jnp.bfloat16)
    padded = jnp.pad(field, ((0, 0), (1, 1), (1, 1), (1, 1)))[:, None]
    cotangent = grad_out.astype(jnp.float32)[:, None]
    taps = lax.conv_general_dilated(padded, cotangent, (1, 1, 1), "VALID", dimension_numbers=("NCDHW", "OIDHW", "CDHWN"), precision=lax.Precision.HIGHEST)
    grad_w = taps.reshape(COUT, 27, CIN)
    return output, grad_w
```

```python
import jax
import jax.numpy as jnp
from jax import lax
from jax.experimental import pallas as pl
from jax.experimental.pallas import tpu as pltpu
from jax.sharding import PartitionSpec as P

F32 = jnp.float32
BF16 = jnp.bfloat16
MESH = pl.DeviceIdType.MESH


def padded_2(block, sides, width):
    for axis, dim in sides:
        count = lax.axis_size(axis)
        forward = [(i, i + 1) for i in range(count - 1)]
        backward = [(target, source) for source, target in forward]
        low = lax.ppermute(
            lax.slice_in_dim(block, block.shape[dim] - width, None, axis=dim), axis, forward
        )
        high = lax.ppermute(lax.slice_in_dim(block, 0, width, axis=dim), axis, backward)
        block = jnp.concatenate([low, block, high], axis=dim)
    return block


def general_body(volume, weights, bias, grad_out):
    channels = volume.shape[0]
    rimmed = padded_2(volume, (("filt", 2), ("depth", 1)), 1)
    padded = jnp.pad(rimmed, ((0, 0), (0, 0), (0, 0), (1, 1)))
    stacked = padded[None]
    per_channel = padded[:, None]
    piece = lax.all_gather(weights, "filt", axis=0, tiled=True)
    count = piece.shape[0]
    kernel = piece.reshape(count, 3, 3, 3, channels)
    result = lax.conv_general_dilated(
        stacked,
        kernel,
        (1, 1, 1),
        "VALID",
        dimension_numbers=("NCDHW", "ODHWI", "NCDHW"),
        preferred_element_type=jnp.float32,
    )
    output = (result[0] + bias[:, None, None, None]).astype(jnp.bfloat16)
    all_filters = grad_out.shape[0]
    taps = lax.conv_general_dilated(
        per_channel,
        grad_out[:, None],
        (1, 1, 1),
        "VALID",
        dimension_numbers=("NCDHW", "OIDHW", "CDHWN"),
        preferred_element_type=jnp.float32,
    )
    term = taps.reshape(all_filters, 27, channels)
    summed = lax.psum(term, "depth")
    grad_w = lax.psum_scatter(summed, "filt", scatter_dimension=0, tiled=True)
    return (output, grad_w)


def fused_kernel(
    v_ref, w_ref, b_ref, g_ref,
    out_ref, gw_ref,
    vp, g3, wg, w9, part, ra, b1, b2, b3, gs,
    hs, hr, ws, wr, rs_s, rs_r, zs, zr,
):
    me = lax.axis_index("filt")
    core = lax.axis_index("depth")
    other = 1 - core
    xi = me % 2
    yi = (me // 2) % 2
    zi = me // 4
    x_peer = me + 1 - 2 * xi
    y_peer = me + 2 - 4 * yi
    z_to = [(zi + k) % 4 for k in (1, 2, 3)]
    z_peer = [t * 4 + yi * 2 + xi for t in z_to]
    left, right = me - 1, me + 1

    def dev(filt, depth=None):
        return {"filt": filt, "depth": core if depth is None else depth}

    def copy(src, dst, s_sem, r_sem, device):
        return pltpu.make_async_remote_copy(
            src_ref=src, dst_ref=dst, send_sem=s_sem, recv_sem=r_sem,
            device_id=device, device_id_type=MESH,
        )

    barrier = pltpu.get_barrier_semaphore()

    def greet(device):
        pl.semaphore_signal(barrier, inc=1, device_id=device, device_id_type=MESH)

    greet(dev(me, other))
    greet(dev(x_peer))
    greet(dev(y_peer))
    for p in z_peer:
        greet(dev(p))

    @pl.when(me > 0)
    def _():
        greet(dev(left))

    @pl.when(me < 15)
    def _():
        greet(dev(right))

    pl.semaphore_wait(barrier, 6 + jnp.minimum(me, 1) + jnp.minimum(15 - me, 1))

    to_right = copy(v_ref.at[:, :, 384:512], vp.at[1:5, :, 0:128], hs.at[0], hr.at[0], dev(right))
    to_left = copy(v_ref.at[:, :, 0:128], vp.at[1:5, :, 640:768], hs.at[1], hr.at[1], dev(left))

    @pl.when(me < 15)
    def _():
        to_right.start()

    @pl.when(me > 0)
    def _():
        to_left.start()

    my_edge = 3 - 3 * core
    there = 5 * core
    send_slot = 5 - 5 * other
    inner = copy(v_ref.at[my_edge], vp.at[send_slot, :, 128:640], hs.at[2], hr.at[2], dev(me, other))
    inner.start()

    wg[core, zi, yi, xi] = w_ref[core]
    for k in range(3):
        copy(w_ref.at[core], wg.at[core, zi, yi, xi], ws.at[k], wr.at[k], dev(z_peer[k])).start()

    vp[1:5, :, 128:640] = v_ref[...]
    empty = 5 - 5 * (1 - core)
    vp[empty] = jnp.zeros((256, 768), BF16)

    @pl.when(me == 0)
    def _():
        vp[1:5, :, 0:128] = jnp.zeros((4, 256, 128), BF16)
        vp[send_zero_slot(core), :, 0:128] = jnp.zeros((256, 128), BF16)

    @pl.when(me == 15)
    def _():
        vp[1:5, :, 640:768] = jnp.zeros((4, 256, 128), BF16)
        vp[send_zero_slot(core), :, 640:768] = jnp.zeros((256, 128), BF16)

    lane = lax.broadcasted_iota(jnp.int32, (128, 128), 1)
    for z in range(4):
        for x in range(4):
            cols = slice(x * 128, x * 128 + 128)
            g = g_ref[z, :, cols]
            gf = g.astype(F32)
            up = jnp.where(lane == 127, 0.0, pltpu.roll(gf, 127, 1))
            down = jnp.where(lane == 0, 0.0, pltpu.roll(gf, 1, 1))
            g3[z, 0:128, cols] = up.astype(BF16)
            g3[z, 128:256, cols] = g
            g3[z, 256:384, cols] = down.astype(BF16)

    edge_slot = 4 - 3 * core
    corner_l = copy(vp.at[edge_slot, :, 0:128], vp.at[send_slot, :, 0:128], hs.at[3], hr.at[3], dev(me, other))
    corner_r = copy(vp.at[edge_slot, :, 640:768], vp.at[send_slot, :, 640:768], hs.at[4], hr.at[4], dev(me, other))

    @pl.when(me > 0)
    def _():
        to_right.wait_recv()
        corner_l.start()

    @pl.when(me < 15)
    def _():
        to_left.wait_recv()
        corner_r.start()

    w_z = [copy(w_ref.at[core], wg.at[core, zi, yi, xi], ws.at[k], wr.at[k], dev(z_peer[k])) for k in range(3)]
    for c in w_z:
        c.wait_recv()
    w_y = copy(wg.at[core, :, yi, xi], wg.at[core, :, yi, xi], ws.at[3], wr.at[3], dev(y_peer))
    w_y.start()
    w_x = copy(wg.at[core, :, :, xi], wg.at[core, :, :, xi], ws.at[4], wr.at[4], dev(x_peer))
    w_c = copy(wg.at[core], wg.at[core], ws.at[5], wr.at[5], dev(me, other))

    inner.wait_recv()

    @pl.when(me > 0)
    def _():
        corner_l.wait_recv()

    @pl.when(me < 15)
    def _():
        corner_r.wait_recv()

    def grad(j):
        dz, dx = j // 3, j % 3
        total = None
        for z in range(4):
            term = lax.dot_general(
                g3[z], vp[z + dz, :, dx * 128 : dx * 128 + 512],
                (((1,), (1,)), ((), ())), preferred_element_type=F32,
            )
            total = term if total is None else total + term
        for h in range(2):
            part[j, h] = total[:, h * 128 : h * 128 + 128].reshape(3, 4, 2, 2, 8, 128)

    def stage_a(j):
        return copy(part.at[j, other], ra.at[j], rs_s.at[0, j], rs_r.at[0, j], dev(me, other))

    def stage_1(j):
        if j % 2 == 0:
            return copy(ra.at[j, :, :, :, 1 - xi], b1.at[j], rs_s.at[1, j], rs_r.at[1, j], dev(x_peer))
        return copy(ra.at[j, :, :, 1 - yi], b1.at[j], rs_s.at[1, j], rs_r.at[1, j], dev(y_peer))

    def stage_2(j):
        if j % 2 == 0:
            return copy(b1.at[j, :, :, 1 - yi], b2.at[j], rs_s.at[2, j], rs_r.at[2, j], dev(y_peer))
        return copy(b1.at[j, :, :, 1 - xi], b2.at[j], rs_s.at[2, j], rs_r.at[2, j], dev(x_peer))

    def stage_3(j):
        return [
            copy(b2.at[j, :, z_to[k]], b3.at[j, k], zs.at[j, k], zr.at[j, k], dev(z_peer[k]))
            for k in range(3)
        ]

    def after_a(j):
        stage_a(j).wait_recv()
        ra[j] = ra[j] + part[j, core]
        stage_1(j).start()

    def after_1(j):
        stage_1(j).wait_recv()
        mine = ra[j, :, :, :, xi] if j % 2 == 0 else ra[j, :, :, yi]
        b1[j] = b1[j] + mine
        stage_2(j).start()

    def after_2(j):
        stage_2(j).wait_recv()
        mine = b1[j, :, :, yi] if j % 2 == 0 else b1[j, :, :, xi]
        b2[j] = b2[j] + mine
        for c in stage_3(j):
            c.start()

    def after_3(j):
        for c in stage_3(j):
            c.wait_recv()
        gs[core, 3 * j : 3 * j + 3] = b2[j, :, zi] + b3[j, 0] + b3[j, 1] + b3[j, 2]

    def arrange():
        for h in range(2):
            for z in range(4):
                for y in range(2):
                    pair = [wg[h, z, y, x].astype(F32).reshape(27, 8, 128) for x in range(2)]
                    rows = jnp.concatenate(pair, axis=1).astype(BF16).reshape(9, 3, 16, 128)
                    at = 16 * (2 * z + y)
                    for dy in range(3):
                        w9[:, dy * 128 + at : dy * 128 + at + 16, h * 128 : h * 128 + 128] = rows[:, dy]

    def forward(u):
        z, half = u // 2, u % 2
        total = None
        for dz in range(3):
            for dx in range(3):
                at = (dx + 2 * half) * 128
                term = jnp.dot(w9[dz * 3 + dx], vp[z + dz, :, at : at + 256], preferred_element_type=F32)
                total = term if total is None else total + term
        for x in range(2):
            cols = slice(x * 128, x * 128 + 128)
            low = jnp.where(lane == 0, 0.0, pltpu.roll(total[0:128, cols], 1, 1))
            high = jnp.where(lane == 127, 0.0, pltpu.roll(total[256:384, cols], 127, 1))
            value = low + total[128:256, cols] + high + b_ref[...]
            at = (x + 2 * half) * 128
            out_ref[z, :, at : at + 128] = value.astype(BF16)

    for t in range(9):
        grad(t)
        stage_a(t).start()
        if t >= 1:
            after_a(t - 1)
        if t == 3:
            w_y.wait_recv()
            w_x.start()
        if t >= 5:
            after_1(t - 5)
    after_a(8)
    w_x.wait_recv()
    w_c.start()
    after_1(4)
    after_2(0)
    w_c.wait_recv()
    arrange()
    for u in range(8):
        forward(u)
        if u < 4:
            after_1(5 + u)
        after_2(1 + u)
        if u >= 3:
            after_3(u - 3)
    for j in range(5, 9):
        after_3(j)
    last = copy(gs.at[core], gs.at[core], hs.at[5], hr.at[5], dev(me, other))
    last.start()
    gw_ref[core] = gs[core]

    @pl.when(me < 15)
    def _():
        to_right.wait_send()
        corner_r.wait_send()

    @pl.when(me > 0)
    def _():
        to_left.wait_send()
        corner_l.wait_send()

    inner.wait_send()
    for c in w_z + [w_y, w_x, w_c]:
        c.wait_send()
    for j in range(9):
        stage_a(j).wait_send()
        stage_1(j).wait_send()
        stage_2(j).wait_send()
        for c in stage_3(j):
            c.wait_send()
    last.wait()
    gw_ref[other] = gs[other]


def send_zero_slot(core):
    return 5 - 5 * core


def fused_body(volume, weights, bias, grad_out):
    v = volume.transpose(1, 0, 2, 3).reshape(4, 256, 512)
    g = grad_out.transpose(1, 0, 2, 3).reshape(4, 128, 512)
    w = weights.reshape(8, 27, 2, 128).transpose(2, 1, 0, 3).reshape(2, 216, 128)
    b = jnp.broadcast_to(bias[:, None], (128, 128))
    vmem = pl.BlockSpec(memory_space=pltpu.VMEM)
    dma = pltpu.SemaphoreType.DMA
    out, gw = pl.pallas_call(
        fused_kernel,
        out_shape=(
            jax.ShapeDtypeStruct((4, 128, 512), BF16),
            jax.ShapeDtypeStruct((2, 27, 8, 128), F32),
        ),
        in_specs=[vmem] * 4,
        out_specs=(vmem, vmem),
        scratch_shapes=[
            pltpu.VMEM((6, 256, 768), BF16),
            pltpu.VMEM((4, 384, 512), BF16),
            pltpu.VMEM((2, 4, 2, 2, 216, 128), BF16),
            pltpu.VMEM((9, 384, 256), BF16),
            pltpu.VMEM((9, 2, 3, 4, 2, 2, 8, 128), F32),
            pltpu.VMEM((9, 3, 4, 2, 2, 8, 128), F32),
            pltpu.VMEM((9, 3, 4, 2, 8, 128), F32),
            pltpu.VMEM((9, 3, 4, 8, 128), F32),
            pltpu.VMEM((9, 3, 3, 8, 128), F32),
            pltpu.VMEM((2, 27, 8, 128), F32),
            dma((6,)), dma((6,)), dma((6,)), dma((6,)),
            dma((3, 9)), dma((3, 9)), dma((9, 3)), dma((9, 3)),
        ],
        compiler_params=pltpu.CompilerParams(
            collective_id=0, has_side_effects=True, vmem_limit_bytes=48 << 20
        ),
    )(v, w, b, g)
    output = out.reshape(4, 128, 4, 128).transpose(1, 0, 2, 3)
    grad_w = gw.transpose(2, 1, 0, 3).reshape(8, 27, 256)
    return (output, grad_w)


def solution(mesh):
    in_specs = (
        P(None, "depth", "filt", None),
        P("filt", None, None),
        P(),
        P(None, "depth", "filt", None),
    )
    out_specs = (P(None, "depth", "filt", None), P("filt", None, None))
    small = mesh.shape["filt"] == 16 and mesh.shape["depth"] == 2

    def body(volume, weights, bias, grad_out):
        shapes = (volume.shape, weights.shape, grad_out.shape)
        if small and shapes == ((256, 4, 4, 128), (8, 27, 256), (128, 4, 4, 128)):
            return fused_body(volume, weights, bias, grad_out)
        return general_body(volume, weights, bias, grad_out)

    return jax.shard_map(body, mesh=mesh, in_specs=in_specs, out_specs=out_specs, check_vma=False)
```

```python
import jax
import jax.numpy as jnp
from jax import lax
from jax.experimental import pallas as pl
from jax.experimental.pallas import tpu as pltpu
from jax.sharding import PartitionSpec as P

F32 = jnp.float32
BF16 = jnp.bfloat16
Y_FIRST = (1, 4, 7)
MESH = pl.DeviceIdType.MESH


def padded_2(block, sides, width):
    for axis, dim in sides:
        count = lax.axis_size(axis)
        forward = [(i, i + 1) for i in range(count - 1)]
        backward = [(target, source) for source, target in forward]
        low = lax.ppermute(
            lax.slice_in_dim(block, block.shape[dim] - width, None, axis=dim), axis, forward
        )
        high = lax.ppermute(lax.slice_in_dim(block, 0, width, axis=dim), axis, backward)
        block = jnp.concatenate([low, block, high], axis=dim)
    return block


def general_body(volume, weights, bias, grad_out):
    channels = volume.shape[0]
    rimmed = padded_2(volume, (("filt", 2), ("depth", 1)), 1)
    padded = jnp.pad(rimmed, ((0, 0), (0, 0), (0, 0), (1, 1)))
    stacked = padded[None]
    per_channel = padded[:, None]
    piece = lax.all_gather(weights, "filt", axis=0, tiled=True)
    count = piece.shape[0]
    kernel = piece.reshape(count, 3, 3, 3, channels)
    result = lax.conv_general_dilated(
        stacked,
        kernel,
        (1, 1, 1),
        "VALID",
        dimension_numbers=("NCDHW", "ODHWI", "NCDHW"),
        preferred_element_type=jnp.float32,
    )
    output = (result[0] + bias[:, None, None, None]).astype(jnp.bfloat16)
    all_filters = grad_out.shape[0]
    taps = lax.conv_general_dilated(
        per_channel,
        grad_out[:, None],
        (1, 1, 1),
        "VALID",
        dimension_numbers=("NCDHW", "OIDHW", "CDHWN"),
        preferred_element_type=jnp.float32,
    )
    term = taps.reshape(all_filters, 27, channels)
    summed = lax.psum(term, "depth")
    grad_w = lax.psum_scatter(summed, "filt", scatter_dimension=0, tiled=True)
    return (output, grad_w)


def fused_kernel(
    v_ref, w_ref, b_ref, g_ref,
    out_ref, gw_ref,
    vp, g3, wg, w9, part, ra, b1, b2, b3, gs,
    hs, hr, ws, wr, rs_s, rs_r, zs, zr,
):
    me = lax.axis_index("filt")
    core = lax.axis_index("depth")
    other = 1 - core
    xi = me % 2
    yi = (me // 2) % 2
    zi = me // 4
    x_peer = me + 1 - 2 * xi
    y_peer = me + 2 - 4 * yi
    z_to = [(zi + k) % 4 for k in (1, 2, 3)]
    z_peer = [t * 4 + yi * 2 + xi for t in z_to]
    left, right = me - 1, me + 1

    def dev(filt, depth=None):
        return {"filt": filt, "depth": core if depth is None else depth}

    def copy(src, dst, s_sem, r_sem, device):
        return pltpu.make_async_remote_copy(
            src_ref=src, dst_ref=dst, send_sem=s_sem, recv_sem=r_sem,
            device_id=device, device_id_type=MESH,
        )

    barrier = pltpu.get_barrier_semaphore()

    def greet(device):
        pl.semaphore_signal(barrier, inc=1, device_id=device, device_id_type=MESH)

    greet(dev(me, other))
    greet(dev(x_peer))
    greet(dev(y_peer))
    for p in z_peer:
        greet(dev(p))

    @pl.when(me > 0)
    def _():
        greet(dev(left))

    @pl.when(me < 15)
    def _():
        greet(dev(right))

    pl.semaphore_wait(barrier, 6 + jnp.minimum(me, 1) + jnp.minimum(15 - me, 1))

    w_x = copy(w_ref.at[core], wg.at[core, yi, zi, xi], ws.at[3], wr.at[3], dev(x_peer))
    w_x.start()
    wg[core, yi, zi, xi] = w_ref[core]

    to_right = copy(v_ref.at[:, 3], vp.at[1:5, 0], hs.at[0], hr.at[0], dev(right))
    to_left = copy(v_ref.at[:, 0], vp.at[1:5, 5], hs.at[1], hr.at[1], dev(left))

    @pl.when(me < 15)
    def _():
        to_right.start()

    @pl.when(me > 0)
    def _():
        to_left.start()

    my_edge = 3 - 3 * core
    there = 5 * core
    send_slot = 5 - 5 * other
    inner = copy(v_ref.at[my_edge], vp.at[send_slot, 1:5], hs.at[2], hr.at[2], dev(me, other))
    inner.start()

    vp[1:5, 1:5] = v_ref[...]
    empty = 5 - 5 * (1 - core)
    vp[empty] = jnp.zeros((6, 256, 128), BF16)

    @pl.when(me == 0)
    def _():
        vp[1:5, 0] = jnp.zeros((4, 256, 128), BF16)
        vp[send_zero_slot(core), 0] = jnp.zeros((256, 128), BF16)

    @pl.when(me == 15)
    def _():
        vp[1:5, 5] = jnp.zeros((4, 256, 128), BF16)
        vp[send_zero_slot(core), 5] = jnp.zeros((256, 128), BF16)

    lane = lax.broadcasted_iota(jnp.int32, (128, 128), 1)
    for z in range(4):
        for x in range(4):
            cols = slice(x * 128, x * 128 + 128)
            g = g_ref[z, x]
            gf = g.astype(F32)
            up = jnp.where(lane == 127, 0.0, pltpu.roll(gf, 127, 1))
            down = jnp.where(lane == 0, 0.0, pltpu.roll(gf, 1, 1))
            g3[z, 0:128, cols] = up.astype(BF16)
            g3[z, 128:256, cols] = g
            g3[z, 256:384, cols] = down.astype(BF16)

    w_z = [
        copy(wg.at[core, yi, zi], wg.at[core, yi, zi], ws.at[k], wr.at[k], dev(z_peer[k]))
        for k in range(3)
    ]
    w_y = copy(wg.at[core, yi], wg.at[core, yi], ws.at[4], wr.at[4], dev(y_peer))
    w_c = copy(wg.at[core], wg.at[core], ws.at[5], wr.at[5], dev(me, other))

    def grad(j):
        dz, dx = j // 3, j % 3
        total = None
        for z in range(4):
            term = lax.dot_general(
                g3[z], jnp.concatenate([vp[z + dz, dx + x] for x in range(4)], axis=1),
                (((1,), (1,)), ((), ())), preferred_element_type=F32,
            )
            total = term if total is None else total + term
        for h in range(2):
            blocks = total[:, h * 128 : h * 128 + 128].reshape(3, 4, 2, 2, 8, 128)
            for y in range(2):
                for x in range(2):
                    for dy in range(3):
                        first, second = (x, y) if j not in Y_FIRST else (y, x)
                        part[j, h, first, second, :, dy] = blocks[dy, :, y, x]

    def stage_a(j):
        return copy(part.at[j, other], ra.at[j], rs_s.at[0, j], rs_r.at[0, j], dev(me, other))

    def path(j):
        return ((xi, x_peer), (yi, y_peer)) if j not in Y_FIRST else ((yi, y_peer), (xi, x_peer))

    def stage_1(j):
        side, peer = path(j)[0]
        return copy(ra.at[j, 1 - side], b1.at[j], rs_s.at[1, j], rs_r.at[1, j], dev(peer))

    def stage_2(j):
        side, peer = path(j)[1]
        return copy(b1.at[j, 1 - side], b2.at[j], rs_s.at[2, j], rs_r.at[2, j], dev(peer))

    def stage_3(j):
        return [
            copy(b2.at[j, z_to[k]], b3.at[j, k], zs.at[j, k], zr.at[j, k], dev(z_peer[k]))
            for k in range(3)
        ]

    def after_a(j):
        stage_a(j).wait_recv()
        ra[j] = ra[j] + part[j, core]
        stage_1(j).start()

    def after_1(j):
        stage_1(j).wait_recv()
        b1[j] = b1[j] + ra[j, path(j)[0][0]]
        stage_2(j).start()

    def after_2(j):
        stage_2(j).wait_recv()
        b2[j] = b2[j] + b1[j, path(j)[1][0]]
        for c in stage_3(j):
            c.start()

    def after_3(j):
        for c in stage_3(j):
            c.wait_recv()
        gs[core, 3 * j : 3 * j + 3] = b2[j, zi] + b3[j, 0] + b3[j, 1] + b3[j, 2]

    def arrange():
        for h in range(2):
            for z in range(4):
                for y in range(2):
                    pair = [wg[h, y, z, x].astype(F32).reshape(27, 8, 128) for x in range(2)]
                    rows = jnp.concatenate(pair, axis=1).astype(BF16).reshape(9, 3, 16, 128)
                    at = 16 * (2 * z + y)
                    for dy in range(3):
                        w9[:, dy * 128 + at : dy * 128 + at + 16, h * 128 : h * 128 + 128] = rows[:, dy]

    def forward(u):
        z, half = u // 2, u % 2
        total = None
        for dz in range(3):
            for dx in range(3):
                at = dx + 2 * half
                cells = jnp.concatenate([vp[z + dz, at], vp[z + dz, at + 1]], axis=1)
                term = jnp.dot(w9[dz * 3 + dx], cells, preferred_element_type=F32)
                total = term if total is None else total + term
        for x in range(2):
            cols = slice(x * 128, x * 128 + 128)
            low = jnp.where(lane == 0, 0.0, pltpu.roll(total[0:128, cols], 1, 1))
            high = jnp.where(lane == 127, 0.0, pltpu.roll(total[256:384, cols], 127, 1))
            value = low + total[128:256, cols] + high + b_ref[...]
            out_ref[z, x + 2 * half] = value.astype(BF16)

    edge_slot = 4 - 3 * core
    corner_l = copy(vp.at[edge_slot, 0], vp.at[send_slot, 0], hs.at[3], hr.at[3], dev(me, other))
    corner_r = copy(vp.at[edge_slot, 5], vp.at[send_slot, 5], hs.at[4], hr.at[4], dev(me, other))

    def rim():
        @pl.when(me > 0)
        def _():
            to_right.wait_recv()
            corner_l.start()

        @pl.when(me < 15)
        def _():
            to_left.wait_recv()
            corner_r.start()

    def corners():
        @pl.when(me > 0)
        def _():
            corner_l.wait_recv()

        @pl.when(me < 15)
        def _():
            corner_r.wait_recv()

    def chunk(j):
        grad(j)
        stage_a(j).start()

    w_x.wait_recv()
    for c in w_z:
        c.start()
    inner.wait_recv()
    chunk(1)
    chunk(4)
    after_a(1)
    chunk(7)
    after_a(4)
    after_a(7)
    after_1(1)
    after_1(4)
    rim()
    chunk(3)
    chunk(5)
    after_a(3)
    for c in w_z:
        c.wait_recv()
    w_y.start()
    after_a(5)
    after_1(7)
    corners()
    chunk(0)
    chunk(2)
    after_a(0)
    chunk(6)
    after_a(2)
    chunk(8)
    after_a(6)
    after_a(8)
    after_2(1)
    after_2(4)
    after_1(3)
    after_2(7)
    after_1(5)
    after_3(1)
    after_2(3)
    after_1(0)
    after_2(5)
    after_3(4)
    w_y.wait_recv()
    w_c.start()
    after_1(2)
    after_2(0)
    after_3(7)
    w_c.wait_recv()
    arrange()
    forward(0)
    after_1(6)
    after_2(2)
    after_3(3)
    forward(1)
    forward(2)
    after_1(8)
    after_2(6)
    forward(3)
    after_3(5)
    forward(4)
    after_2(8)
    forward(5)
    after_3(0)
    forward(6)
    after_3(2)
    forward(7)
    after_3(6)
    after_3(8)
    last = copy(gs.at[core], gs.at[core], hs.at[5], hr.at[5], dev(me, other))
    last.start()

    @pl.when(me < 15)
    def _():
        to_right.wait_send()
        corner_r.wait_send()

    @pl.when(me > 0)
    def _():
        to_left.wait_send()
        corner_l.wait_send()

    inner.wait_send()
    for c in w_z + [w_y, w_x, w_c]:
        c.wait_send()
    for j in range(9):
        stage_a(j).wait_send()
        stage_1(j).wait_send()
        stage_2(j).wait_send()
        for c in stage_3(j):
            c.wait_send()
    last.wait()
    for h in range(2):
        gw_ref[:, :, h * 128 : h * 128 + 128] = gs[h]


def send_zero_slot(core):
    return 5 - 5 * core


def fused_body(volume, weights, bias, grad_out):
    v = volume.transpose(1, 2, 0, 3)
    g = grad_out.transpose(1, 2, 0, 3)
    w = weights.reshape(8, 27, 2, 128).transpose(2, 1, 0, 3).reshape(2, 216, 128)
    b = jnp.broadcast_to(bias[:, None], (128, 128))
    vmem = pl.BlockSpec(memory_space=pltpu.VMEM)
    dma = pltpu.SemaphoreType.DMA
    out, gw = pl.pallas_call(
        fused_kernel,
        out_shape=(
            jax.ShapeDtypeStruct((4, 4, 128, 128), BF16),
            jax.ShapeDtypeStruct((27, 8, 256), F32),
        ),
        in_specs=[vmem] * 4,
        out_specs=(vmem, vmem),
        scratch_shapes=[
            pltpu.VMEM((6, 6, 256, 128), BF16),
            pltpu.VMEM((4, 384, 512), BF16),
            pltpu.VMEM((2, 2, 4, 2, 216, 128), BF16),
            pltpu.VMEM((9, 384, 256), BF16),
            pltpu.VMEM((9, 2, 2, 2, 4, 3, 8, 128), F32),
            pltpu.VMEM((9, 2, 2, 4, 3, 8, 128), F32),
            pltpu.VMEM((9, 2, 4, 3, 8, 128), F32),
            pltpu.VMEM((9, 4, 3, 8, 128), F32),
            pltpu.VMEM((9, 3, 3, 8, 128), F32),
            pltpu.VMEM((2, 27, 8, 128), F32),
            dma((6,)), dma((6,)), dma((6,)), dma((6,)),
            dma((3, 9)), dma((3, 9)), dma((9, 3)), dma((9, 3)),
        ],
        compiler_params=pltpu.CompilerParams(
            collective_id=0, has_side_effects=True, vmem_limit_bytes=48 << 20
        ),
    )(v, w, b, g)
    output = out.transpose(2, 0, 1, 3)
    grad_w = gw.transpose(1, 0, 2)
    return (output, grad_w)


def solution(mesh):
    in_specs = (
        P(None, "depth", "filt", None),
        P("filt", None, None),
        P(),
        P(None, "depth", "filt", None),
    )
    out_specs = (P(None, "depth", "filt", None), P("filt", None, None))
    small = mesh.shape["filt"] == 16 and mesh.shape["depth"] == 2

    def body(volume, weights, bias, grad_out):
        shapes = (volume.shape, weights.shape, grad_out.shape)
        if small and shapes == ((256, 4, 4, 128), (8, 27, 256), (128, 4, 4, 128)):
            return fused_body(volume, weights, bias, grad_out)
        return general_body(volume, weights, bias, grad_out)

    return jax.shard_map(body, mesh=mesh, in_specs=in_specs, out_specs=out_specs, check_vma=False)
```

```python
import jax
import jax.numpy as jnp
from jax import lax
from jax.experimental import pallas as pl
from jax.experimental.pallas import tpu as pltpu
from jax.sharding import PartitionSpec as P

F32 = jnp.float32
BF16 = jnp.bfloat16
Y_FIRST = (1, 4, 7)
MESH = pl.DeviceIdType.MESH


def padded_2(block, sides, width):
    for axis, dim in sides:
        count = lax.axis_size(axis)
        forward = [(i, i + 1) for i in range(count - 1)]
        backward = [(target, source) for source, target in forward]
        low = lax.ppermute(
            lax.slice_in_dim(block, block.shape[dim] - width, None, axis=dim), axis, forward
        )
        high = lax.ppermute(lax.slice_in_dim(block, 0, width, axis=dim), axis, backward)
        block = jnp.concatenate([low, block, high], axis=dim)
    return block


def general_body(volume, weights, bias, grad_out):
    channels = volume.shape[0]
    rimmed = padded_2(volume, (("filt", 2), ("depth", 1)), 1)
    padded = jnp.pad(rimmed, ((0, 0), (0, 0), (0, 0), (1, 1)))
    stacked = padded[None]
    per_channel = padded[:, None]
    piece = lax.all_gather(weights, "filt", axis=0, tiled=True)
    count = piece.shape[0]
    kernel = piece.reshape(count, 3, 3, 3, channels)
    result = lax.conv_general_dilated(
        stacked,
        kernel,
        (1, 1, 1),
        "VALID",
        dimension_numbers=("NCDHW", "ODHWI", "NCDHW"),
        preferred_element_type=jnp.float32,
    )
    output = (result[0] + bias[:, None, None, None]).astype(jnp.bfloat16)
    all_filters = grad_out.shape[0]
    taps = lax.conv_general_dilated(
        per_channel,
        grad_out[:, None],
        (1, 1, 1),
        "VALID",
        dimension_numbers=("NCDHW", "OIDHW", "CDHWN"),
        preferred_element_type=jnp.float32,
    )
    term = taps.reshape(all_filters, 27, channels)
    summed = lax.psum(term, "depth")
    grad_w = lax.psum_scatter(summed, "filt", scatter_dimension=0, tiled=True)
    return (output, grad_w)


def fused_kernel(
    v_ref, w_ref, b_ref, g_ref,
    out_ref, gw_ref,
    vp, g3, wg, w9, part, ra, b1, b2, b3, gs,
    hs, hr, ws, wr, rs_s, rs_r, zs, zr,
):
    me = lax.axis_index("filt")
    core = lax.axis_index("depth")
    other = 1 - core
    xi = me % 2
    yi = (me // 2) % 2
    zi = me // 4
    x_peer = me + 1 - 2 * xi
    y_peer = me + 2 - 4 * yi
    z_to = [(zi + k) % 4 for k in (1, 2, 3)]
    z_peer = [t * 4 + yi * 2 + xi for t in z_to]
    left, right = me - 1, me + 1

    def dev(filt, depth=None):
        return {"filt": filt, "depth": core if depth is None else depth}

    def copy(src, dst, s_sem, r_sem, device):
        return pltpu.make_async_remote_copy(
            src_ref=src, dst_ref=dst, send_sem=s_sem, recv_sem=r_sem,
            device_id=device, device_id_type=MESH,
        )

    barrier = pltpu.get_barrier_semaphore()

    def greet(device):
        pl.semaphore_signal(barrier, inc=1, device_id=device, device_id_type=MESH)

    greet(dev(me, other))
    greet(dev(x_peer))
    greet(dev(y_peer))
    for p in z_peer:
        greet(dev(p))

    @pl.when(me > 0)
    def _():
        greet(dev(left))

    @pl.when(me < 15)
    def _():
        greet(dev(right))

    pl.semaphore_wait(barrier, 6 + jnp.minimum(me, 1) + jnp.minimum(15 - me, 1))

    w_x = copy(w_ref.at[core], wg.at[core, yi, zi, xi], ws.at[3], wr.at[3], dev(x_peer))
    w_x.start()
    wg[core, yi, zi, xi] = w_ref[core]

    to_right = copy(v_ref.at[:, 3], vp.at[1:5, 0], hs.at[0], hr.at[0], dev(right))
    to_left = copy(v_ref.at[:, 0], vp.at[1:5, 5], hs.at[1], hr.at[1], dev(left))

    @pl.when(me < 15)
    def _():
        to_right.start()

    @pl.when(me > 0)
    def _():
        to_left.start()

    my_edge = 3 - 3 * core
    there = 5 * core
    send_slot = 5 - 5 * other
    inner = copy(v_ref.at[my_edge], vp.at[send_slot, 1:5], hs.at[2], hr.at[2], dev(me, other))
    inner.start()

    vp[1:5, 1:5] = v_ref[...]
    empty = 5 - 5 * (1 - core)
    vp[empty] = jnp.zeros((6, 256, 128), BF16)

    @pl.when(me == 0)
    def _():
        vp[1:5, 0] = jnp.zeros((4, 256, 128), BF16)
        vp[send_zero_slot(core), 0] = jnp.zeros((256, 128), BF16)

    @pl.when(me == 15)
    def _():
        vp[1:5, 5] = jnp.zeros((4, 256, 128), BF16)
        vp[send_zero_slot(core), 5] = jnp.zeros((256, 128), BF16)

    lane = lax.broadcasted_iota(jnp.int32, (128, 128), 1)
    for z in range(4):
        for x in range(4):
            cols = slice(x * 128, x * 128 + 128)
            g = g_ref[z, x]
            gf = g.astype(F32)
            up = jnp.where(lane == 127, 0.0, pltpu.roll(gf, 127, 1))
            down = jnp.where(lane == 0, 0.0, pltpu.roll(gf, 1, 1))
            g3[z, 0:128, cols] = up.astype(BF16)
            g3[z, 128:256, cols] = g
            g3[z, 256:384, cols] = down.astype(BF16)

    w_z = [
        copy(wg.at[core, yi, zi], wg.at[core, yi, zi], ws.at[k], wr.at[k], dev(z_peer[k]))
        for k in range(3)
    ]
    w_y = copy(wg.at[core, yi], wg.at[core, yi], ws.at[4], wr.at[4], dev(y_peer))
    w_c = [
        copy(wg.at[core, row], wg.at[core, row], ws.at[5 + k], wr.at[5 + k], dev(me, other))
        for k, row in enumerate((yi, 1 - yi))
    ]

    def grad(j):
        dz, dx = j // 3, j % 3
        total = None
        for z in range(4):
            term = lax.dot_general(
                g3[z], jnp.concatenate([vp[z + dz, dx + x] for x in range(4)], axis=1),
                (((1,), (1,)), ((), ())), preferred_element_type=F32,
            )
            total = term if total is None else total + term
        for h in range(2):
            blocks = total[:, h * 128 : h * 128 + 128].reshape(3, 4, 2, 2, 8, 128)
            for y in range(2):
                for x in range(2):
                    for dy in range(3):
                        first, second = (x, y) if j not in Y_FIRST else (y, x)
                        part[j, h, first, second, :, dy] = blocks[dy, :, y, x]

    def stage_a(j):
        return copy(part.at[j, other], ra.at[j], rs_s.at[0, j], rs_r.at[0, j], dev(me, other))

    def path(j):
        return ((xi, x_peer), (yi, y_peer)) if j not in Y_FIRST else ((yi, y_peer), (xi, x_peer))

    def stage_1(j):
        side, peer = path(j)[0]
        return copy(ra.at[j, 1 - side], b1.at[j], rs_s.at[1, j], rs_r.at[1, j], dev(peer))

    def stage_2(j):
        side, peer = path(j)[1]
        return copy(b1.at[j, 1 - side], b2.at[j], rs_s.at[2, j], rs_r.at[2, j], dev(peer))

    def stage_3(j):
        return [
            copy(b2.at[j, z_to[k]], b3.at[j, k], zs.at[j, k], zr.at[j, k], dev(z_peer[k]))
            for k in range(3)
        ]

    def after_a(j):
        stage_a(j).wait_recv()
        ra[j] = ra[j] + part[j, core]
        stage_1(j).start()

    def after_1(j):
        stage_1(j).wait_recv()
        b1[j] = b1[j] + ra[j, path(j)[0][0]]
        stage_2(j).start()

    def after_2(j):
        stage_2(j).wait_recv()
        b2[j] = b2[j] + b1[j, path(j)[1][0]]
        for c in stage_3(j):
            c.start()

    def after_3(j):
        for c in stage_3(j):
            c.wait_recv()
        gs[core, 3 * j : 3 * j + 3] = b2[j, zi] + b3[j, 0] + b3[j, 1] + b3[j, 2]

    def arrange():
        for h in range(2):
            for z in range(4):
                for y in range(2):
                    pair = [wg[h, y, z, x].astype(F32).reshape(27, 8, 128) for x in range(2)]
                    rows = jnp.concatenate(pair, axis=1).astype(BF16).reshape(9, 3, 16, 128)
                    at = 16 * (2 * z + y)
                    for dy in range(3):
                        w9[:, dy * 128 + at : dy * 128 + at + 16, h * 128 : h * 128 + 128] = rows[:, dy]

    def forward(u):
        z, half = u // 2, u % 2
        total = None
        for dz in range(3):
            for dx in range(3):
                at = dx + 2 * half
                cells = jnp.concatenate([vp[z + dz, at], vp[z + dz, at + 1]], axis=1)
                term = jnp.dot(w9[dz * 3 + dx], cells, preferred_element_type=F32)
                total = term if total is None else total + term
        for x in range(2):
            cols = slice(x * 128, x * 128 + 128)
            low = jnp.where(lane == 0, 0.0, pltpu.roll(total[0:128, cols], 1, 1))
            high = jnp.where(lane == 127, 0.0, pltpu.roll(total[256:384, cols], 127, 1))
            value = low + total[128:256, cols] + high + b_ref[...]
            out_ref[z, x + 2 * half] = value.astype(BF16)

    edge_slot = 4 - 3 * core
    corner_l = copy(vp.at[edge_slot, 0], vp.at[send_slot, 0], hs.at[3], hr.at[3], dev(me, other))
    corner_r = copy(vp.at[edge_slot, 5], vp.at[send_slot, 5], hs.at[4], hr.at[4], dev(me, other))

    def rim():
        @pl.when(me > 0)
        def _():
            to_right.wait_recv()
            corner_l.start()

        @pl.when(me < 15)
        def _():
            to_left.wait_recv()
            corner_r.start()

    def corners():
        @pl.when(me > 0)
        def _():
            corner_l.wait_recv()

        @pl.when(me < 15)
        def _():
            corner_r.wait_recv()

    def chunk(j):
        grad(j)
        stage_a(j).start()

    w_x.wait_recv()
    for c in w_z:
        c.start()
    inner.wait_recv()
    chunk(1)
    chunk(4)
    after_a(1)
    chunk(7)
    after_a(4)
    after_a(7)
    after_1(1)
    after_1(4)
    rim()
    chunk(3)
    chunk(5)
    after_a(3)
    for c in w_z:
        c.wait_recv()
    w_y.start()
    w_c[0].start()
    after_a(5)
    after_1(7)
    corners()
    chunk(0)
    chunk(2)
    after_a(0)
    chunk(6)
    after_a(2)
    chunk(8)
    after_a(6)
    after_a(8)
    after_2(1)
    after_2(4)
    after_1(3)
    after_2(7)
    after_1(5)
    after_3(1)
    after_2(3)
    after_1(0)
    after_2(5)
    after_3(4)
    w_y.wait_recv()
    w_c[1].start()
    after_1(2)
    after_2(0)
    after_3(7)
    for c in w_c:
        c.wait_recv()
    arrange()
    forward(0)
    after_1(6)
    after_2(2)
    after_3(3)
    forward(1)
    forward(2)
    after_1(8)
    after_2(6)
    forward(3)
    after_3(5)
    forward(4)
    after_2(8)
    forward(5)
    after_3(0)
    forward(6)
    after_3(2)
    forward(7)
    after_3(6)
    after_3(8)
    last = copy(gs.at[core], gs.at[core], hs.at[5], hr.at[5], dev(me, other))
    last.start()

    @pl.when(me < 15)
    def _():
        to_right.wait_send()
        corner_r.wait_send()

    @pl.when(me > 0)
    def _():
        to_left.wait_send()
        corner_l.wait_send()

    inner.wait_send()
    for c in w_z + [w_y, w_x] + w_c:
        c.wait_send()
    for j in range(9):
        stage_a(j).wait_send()
        stage_1(j).wait_send()
        stage_2(j).wait_send()
        for c in stage_3(j):
            c.wait_send()
    last.wait()
    for h in range(2):
        gw_ref[:, :, h * 128 : h * 128 + 128] = gs[h]


def send_zero_slot(core):
    return 5 - 5 * core


def fused_body(volume, weights, bias, grad_out):
    v = volume.transpose(1, 2, 0, 3)
    g = grad_out.transpose(1, 2, 0, 3)
    w = weights.reshape(8, 27, 2, 128).transpose(2, 1, 0, 3).reshape(2, 216, 128)
    b = jnp.broadcast_to(bias[:, None], (128, 128))
    vmem = pl.BlockSpec(memory_space=pltpu.VMEM)
    dma = pltpu.SemaphoreType.DMA
    out, gw = pl.pallas_call(
        fused_kernel,
        out_shape=(
            jax.ShapeDtypeStruct((4, 4, 128, 128), BF16),
            jax.ShapeDtypeStruct((27, 8, 256), F32),
        ),
        in_specs=[vmem] * 4,
        out_specs=(vmem, vmem),
        scratch_shapes=[
            pltpu.VMEM((6, 6, 256, 128), BF16),
            pltpu.VMEM((4, 384, 512), BF16),
            pltpu.VMEM((2, 2, 4, 2, 216, 128), BF16),
            pltpu.VMEM((9, 384, 256), BF16),
            pltpu.VMEM((9, 2, 2, 2, 4, 3, 8, 128), F32),
            pltpu.VMEM((9, 2, 2, 4, 3, 8, 128), F32),
            pltpu.VMEM((9, 2, 4, 3, 8, 128), F32),
            pltpu.VMEM((9, 4, 3, 8, 128), F32),
            pltpu.VMEM((9, 3, 3, 8, 128), F32),
            pltpu.VMEM((2, 27, 8, 128), F32),
            dma((6,)), dma((6,)), dma((7,)), dma((7,)),
            dma((3, 9)), dma((3, 9)), dma((9, 3)), dma((9, 3)),
        ],
        compiler_params=pltpu.CompilerParams(
            collective_id=0, has_side_effects=True, vmem_limit_bytes=48 << 20
        ),
    )(v, w, b, g)
    output = out.transpose(2, 0, 1, 3)
    grad_w = gw.transpose(1, 0, 2)
    return (output, grad_w)


def solution(mesh):
    in_specs = (
        P(None, "depth", "filt", None),
        P("filt", None, None),
        P(),
        P(None, "depth", "filt", None),
    )
    out_specs = (P(None, "depth", "filt", None), P("filt", None, None))
    small = mesh.shape["filt"] == 16 and mesh.shape["depth"] == 2

    def body(volume, weights, bias, grad_out):
        shapes = (volume.shape, weights.shape, grad_out.shape)
        if small and shapes == ((256, 4, 4, 128), (8, 27, 256), (128, 4, 4, 128)):
            return fused_body(volume, weights, bias, grad_out)
        return general_body(volume, weights, bias, grad_out)

    return jax.shard_map(body, mesh=mesh, in_specs=in_specs, out_specs=out_specs, check_vma=False)
```
